32 devices in a mesh: ctx: 4 (over z), tp: 8 (over y, x, core).
Axes of the slice: x: 2, y: 2, z: 4, core: 2. Of those that a mesh axis runs over, the one named last changes fastest.
Arguments:
- token_ids: int32 [2048], P('ctx'), may hold values from 0 to 200063
- marks: int32 [2048], P('ctx'), may hold values 0 or 1
- table: bfloat16 [256, 3072], P(None, 'tp'), may hold values from -6 to 6
- norm_gain: bfloat16 [3072], replicated, may hold values from 0.099609375 to 1.8984375
- w_query: bfloat16 [3072, 4096], P(None, 'tp'), may hold values from -0.109375 to 0.109375
- w_key: bfloat16 [3072, 4096], P(None, 'tp'), may hold values from -0.109375 to 0.109375
- w_value: bfloat16 [3072, 4096], P(None, 'tp'), may hold values from -0.109375 to 0.109375
- decay_idx: int32 [32], P('tp'), may hold values from 21 to 84
- out_gain: bfloat16 [4096], P('tp'), may hold values from 0.099609375 to 1.8984375
- w_out: bfloat16 [4096, 3072], P('tp'), may hold values from -0.125 to 0.125
Outputs:
- mixed: bfloat16 [2048, 3072], P('ctx', 'tp')
The draws below stay inside these ranges and needn't reach their ends.
All inputs are finite; a program needn't handle non-finite values. No bound on the sum of `marks` on one device may be relied on, other than what follows from the above.
Results may differ from the reference program's by a relative error of at most 0.014.
Values may be sent and summed in bfloat16 or wider, within the bound.
A program may use at most 128 MiB of HBM per device.

```python
import math
import jax
import jax.numpy as jnp
import numpy as np
from jax import lax

D = 3072
HEADS = 32
HEAD_DIM = 128
BUCKETS = 256
VOCAB = 200064
TOK_DEV = 512
TOKENS = 2048
N_CTX = 4
N_TP = 8


def set_ends(array, stream_key, low, largest):
    extent = array.shape
    spot = [jax.random.randint(jax.random.fold_in(stream_key, axis), (), 0, extent[axis]) for axis in range(len(extent))]
    array = array.at[tuple(spot)].set(low)
    longest = extent.index(max(extent))
    spot[longest] = (spot[longest] + 1) % extent[longest]
    return array.at[tuple(spot)].set(largest)


def raised(drawn, rng, source, target, blocks, factor):
    def block_of(axis_at):
        return (jnp.arange(drawn.shape[axis_at]) // (drawn.shape[axis_at] // blocks)).reshape((-1,) + (1,) * (drawn.ndim - 1 - axis_at))

    one_side = jax.random.permutation(rng, blocks)[block_of(target)]
    second = (block_of(target) + blocks // 2) % blocks
    return jnp.where((block_of(source) == one_side) | (block_of(source) == second), factor * drawn, drawn)


def block_levels(stream_key, dims, split, least, top_value):
    gain, own = 1.0, jax.random.fold_in(stream_key, 6)
    for dim, shards_of in split:
        heights = jnp.exp(jax.random.uniform(jax.random.fold_in(own, dim), (shards_of,), jnp.float32, least / len(split), top_value / len(split)))
        gain = gain * jnp.repeat(heights, dims[dim] // shards_of).reshape([-1 if axis == dim else 1 for axis in range(len(dims))])
    return gain


def ranked_wide(own_key, extent, count, slope):
    loads = [min(1 << octave, count + 1 - (1 << octave)) * (1 << 20) // math.isqrt((1 << octave) ** slope) + 1 for octave in range((count + 1).bit_length()) if 1 << octave <= count]
    width = 1 + sum(loads) // (1 << 30)
    grid = np.cumsum(np.array([max(1, weight // width) for weight in loads]))
    ticket = jax.random.randint(jax.random.fold_in(own_key, 1), extent, 0, int(grid[len(loads) - 1]))
    start = jnp.left_shift(1, jnp.searchsorted(jnp.asarray(grid, jnp.int32), ticket, side="right").astype(jnp.int32))
    grade = start - 1 + jax.random.randint(jax.random.fold_in(own_key, 4), extent, 0, 1 << 30) % jnp.minimum(start, count + 1 - start)
    return jax.random.permutation(jax.random.fold_in(own_key, 2), count)[grade].astype(jnp.int32)


def scatter_about(own_key, dims, spread, most, split=(), held_as=jnp.bfloat16):
    entries = jax.random.normal(own_key, dims, jnp.float32) * spread
    if len(split) > 0:
        entries = block_levels(own_key, dims, split, -0.22, 0.18) * entries
    return jnp.clip(entries, min=-most, max=most).astype(held_as)


def bell_draw_with(rng, dims, width, most, split, heavy, kind=jnp.bfloat16):
    values = width * jax.random.normal(rng, dims, jnp.float32)
    if split:
        values = values * block_levels(rng, dims, split, -0.22, 0.18)
    return jnp.clip(raised(values, jax.random.fold_in(rng, 3), *heavy), -most, most).astype(kind)


def setup_inputs(seed: int = 0) -> dict:
    arg_keys = jax.random.split(jax.random.key(seed), 11)
    return {
        "token_ids": set_ends(ranked_wide(arg_keys[0], (TOKENS,), VOCAB, 2), jax.random.fold_in(arg_keys[0], 3), 0, VOCAB - 1).astype(jnp.int32),
        "marks": set_ends((jax.random.randint(arg_keys[1], (TOKENS,), 0, 8 * TOK_DEV) < 1).astype(jnp.int32), jax.random.fold_in(arg_keys[1], 1), 0, 1),
        "table": scatter_about(arg_keys[2], (BUCKETS, D), 1.0, 6.0, ((1, 8),)),
        "norm_gain": jnp.clip(1.0 + 0.18 * jax.random.normal(arg_keys[3], (D,), jnp.float32), 0.099609375, 1.8984375).astype(jnp.bfloat16),
        "w_query": scatter_about(arg_keys[4], (D, HEADS * HEAD_DIM), D ** -0.5, 0.109375, ((1, 8),)),
        "w_key": scatter_about(arg_keys[5], (D, HEADS * HEAD_DIM), D ** -0.5, 0.109375, ((1, 8),)),
        "w_value": scatter_about(arg_keys[6], (D, HEADS * HEAD_DIM), D ** -0.5, 0.109375, ((1, 8),)),
        "decay_idx": set_ends(jax.random.randint(arg_keys[7], (HEADS,), 21, 85), jax.random.fold_in(arg_keys[7], 1), 21, 84).astype(jnp.int32),
        "out_gain": jnp.clip(1.0 + 0.18 * jax.random.normal(arg_keys[8], (HEADS * HEAD_DIM,), jnp.float32), 0.099609375, 1.8984375).astype(jnp.bfloat16),
        "w_out": bell_draw_with(arg_keys[9], (HEADS * HEAD_DIM, D), (HEADS * HEAD_DIM) ** -0.5, 0.125, ((0, 8),), (0, 1, 8, 2.0)),
    }


mark_keep = 0.75

def reference(token_ids, marks, table, norm_gain, w_query, w_key, w_value, decay_idx, out_gain, w_out):
    buckets = table.shape[0]
    head_count = decay_idx.shape[0]
    head_width = w_query.shape[1] // head_count
    model_width = table.shape[1]
    group_width = w_out.shape[0] // N_TP
    base_rate = -jnp.exp2(-0.25 * decay_idx.astype(jnp.float32))
    causal = jnp.arange(TOK_DEV)[:, None] >= jnp.arange(TOK_DEV)[None, :]
    out_groups = w_out.reshape(N_TP, group_width, model_width).astype(jnp.float32)

    def block_step(carried_state, pieces):
        block_ids, block_marks = pieces
        hashed = (block_ids * 7919 + 13) % buckets
        embedded = jnp.take(table, hashed, axis=0)
        x_float = embedded.astype(jnp.float32)
        inv_rms = lax.rsqrt(lax.optimization_barrier(jnp.mean(x_float * x_float, axis=1, keepdims=True)) + 1e-05)
        normed = (x_float * inv_rms * norm_gain.astype(jnp.float32)).astype(jnp.bfloat16)
        query_rows = jax.nn.silu(jnp.dot(normed, w_query, preferred_element_type=jnp.float32)).astype(jnp.bfloat16).reshape(TOK_DEV, head_count, head_width)
        key_rows = jax.nn.silu(jnp.dot(normed, w_key, preferred_element_type=jnp.float32)).astype(jnp.bfloat16).reshape(TOK_DEV, head_count, head_width)
        value_rows = jnp.dot(normed, w_value, preferred_element_type=jnp.float32).astype(jnp.bfloat16).reshape(TOK_DEV, head_count, head_width)
        log_decay = base_rate[None, :] + block_marks.astype(jnp.float32)[:, None] * math.log(mark_keep)
        cumulative = jnp.cumsum(log_decay, axis=0)
        per_head = cumulative.T
        gaps_log = per_head[:, :, None] - per_head[:, None, :]
        decay_mask = jnp.where(causal[None], jnp.exp(jnp.minimum(gaps_log, 0.0)), 0.0)
        scores = jnp.einsum('thd,shd->hts', query_rows.astype(jnp.float32), key_rows.astype(jnp.float32))
        weights = (scores * decay_mask).astype(jnp.bfloat16)
        intra_part = jnp.einsum('hts,shd->thd', weights.astype(jnp.float32), value_rows.astype(jnp.float32))
        carried = jnp.einsum('thd,hde->the', query_rows.astype(jnp.float32), carried_state, precision=lax.Precision.HIGHEST)
        attended = intra_part + jnp.exp(cumulative)[:, :, None] * carried
        out_scale = lax.rsqrt(lax.optimization_barrier(jnp.mean(attended * attended, axis=2, keepdims=True)) + 1e-06)
        normal_out = (attended * out_scale * out_gain.astype(jnp.float32).reshape(head_count, head_width)).astype(jnp.bfloat16)
        grouped = normal_out.reshape(TOK_DEV, N_TP, group_width).astype(jnp.float32)
        partial_value = jnp.einsum('tgc,gcm->gtm', grouped, out_groups).astype(jnp.bfloat16)
        summed = lax.optimization_barrier(jnp.sum(partial_value.astype(jnp.float32), axis=0))
        result = (x_float + summed).astype(jnp.bfloat16)
        block_decay = cumulative[-1]
        decayed = (key_rows.astype(jnp.float32) * jnp.exp(block_decay[None, :] - cumulative)[:, :, None]).astype(jnp.bfloat16)
        local_state = jnp.einsum('shd,she->hde', decayed.astype(jnp.float32), value_rows.astype(jnp.float32))
        next_state = jnp.exp(block_decay)[:, None, None] * carried_state + local_state
        return (next_state, result)
    start_state = jnp.zeros((head_count, head_width, head_width), jnp.float32)
    _, results = lax.scan(block_step, start_state, (token_ids.reshape(N_CTX, TOK_DEV), marks.reshape(N_CTX, TOK_DEV)))
    return results.reshape(N_CTX * TOK_DEV, model_width)
```

```python
import functools
import math

import jax
import jax.numpy as jnp
from jax import lax
from jax.experimental import pallas as pl
from jax.experimental.pallas import tpu as pltpu
from jax.sharding import PartitionSpec as P

MESH = pl.DeviceIdType.MESH
LOG_KEEP = math.log(0.75)
F32, BF16 = jnp.float32, jnp.bfloat16
ORDER = (1, 3, 5, 7, 0, 2, 4, 6)


def dot(a, b):
    return jnp.dot(a, b, preferred_element_type=F32)


def dot_rows(a, b):
    return lax.dot_general(a, b, (((0,), (0,)), ((), ())), preferred_element_type=F32)


def dot_lanes(a, b):
    return lax.dot_general(a, b, (((1,), (1,)), ((), ())), preferred_element_type=F32)


def layer(
    n_ctx, chunk,
    ids_ref, marks_ref, table_ref, gain_ref, wq_ref, wk_ref, wv_ref, idx_ref, ogain_ref, wout_ref,
    out_ref,
    full, normed, w_in, w_o, qkv, hot, state, msg, msgs, att, keep0, s0, r0, keep1, s1, r1, keep2, s2, r2,
    load_sem, ag_send, ag_recv, ctx_send, ctx_recv, rs_send, rs_recv,
):
    me, place = lax.axis_index("tp"), lax.axis_index("ctx")
    buckets, width = table_ref.shape
    rows = ids_ref.shape[1]
    tiles, model, tile = w_in.shape
    heads, hw = state.shape[0], state.shape[1]
    per = tile // hw
    group = heads // per
    bits = [(me // (1 << k)) % 2 for k in range(3)]

    def other(p):
        index = me
        for k in range(3):
            if (p >> k) & 1:
                index = index + (1 - 2 * bits[k]) * (1 << k)
        return index

    sib, xp, yp, diag = other(1), other(2), other(4), other(6)

    loads = []
    for n in range(tiles):
        source = (wq_ref, wk_ref, wv_ref)[n // group]
        loads.append(pltpu.make_async_copy(
            source.at[:, pl.ds((n % group) * tile, tile)], w_in.at[n], load_sem.at[n]))
    for at, p in enumerate(ORDER):
        first = pl.multiple_of(other(p) * width, 128)
        loads.append(pltpu.make_async_copy(
            wout_ref.at[:, pl.ds(first, width)],
            w_o.at[at // 2, :, pl.ds((at % 2) * width, width)], load_sem.at[tiles + at]))
    for load in loads:
        load.start()

    barrier = pltpu.get_barrier_semaphore()
    for peer in (sib, xp, yp):
        pl.semaphore_signal(barrier, inc=1, device_id={"tp": peer}, device_id_type=MESH)
    for d in range(1, n_ctx):
        pl.semaphore_signal(
            barrier, inc=1, device_id={"ctx": lax.rem(place + d, n_ctx)}, device_id_type=MESH)
    pl.semaphore_wait(barrier, 3 + n_ctx - 1)

    half = buckets // 2
    lo, hi = pl.ds(0, half), pl.ds(half, half)

    def ag(k, src, dst, peer):
        return pltpu.make_async_remote_copy(
            src_ref=src, dst_ref=dst, send_sem=ag_send.at[k], recv_sem=ag_recv.at[k],
            device_id={"tp": peer}, device_id_type=MESH)

    gathers = [
        ag(0, table_ref.at[lo], full.at[me, lo], xp),
        ag(1, table_ref.at[hi], full.at[me, hi], yp),
        ag(2, table_ref, full.at[me], sib),
        ag(3, table_ref.at[hi], full.at[me, hi], xp),
        ag(4, table_ref.at[lo], full.at[me, lo], yp),
        ag(5, full.at[xp, lo], full.at[xp, lo], yp),
        ag(6, full.at[yp, hi], full.at[yp, hi], xp),
        ag(7, full.at[xp, lo], full.at[xp, lo], sib),
        ag(8, full.at[yp, hi], full.at[yp, hi], sib),
        ag(9, full.at[xp, hi], full.at[xp, hi], sib),
        ag(10, full.at[yp, lo], full.at[yp, lo], sib),
        ag(11, full.at[diag, lo], full.at[diag, lo], sib),
        ag(12, full.at[diag, hi], full.at[diag, hi], sib),
    ]
    for k in range(5):
        gathers[k].start()
    full[me] = table_ref[...]

    hashed = ((ids_ref[...] * 7919 + 13) & (buckets - 1)).astype(F32)
    upto = lax.broadcasted_iota(jnp.int32, (rows, rows), 0) <= lax.broadcasted_iota(
        jnp.int32, (rows, rows), 1)
    mark8 = jnp.broadcast_to(marks_ref[...].astype(F32), (8, rows)).astype(BF16)
    count = dot(mark8, jnp.where(upto, 1.0, 0.0).astype(BF16))
    sub = lax.broadcasted_iota(jnp.int32, (8, rows), 0)
    turned = jnp.where(sub == 0, jnp.broadcast_to(hashed, (8, rows)), count).T
    hash_col, count_col = turned[:, 0:1], turned[:, 1:2]
    hot[...] = jnp.where(
        lax.broadcasted_iota(jnp.int32, (rows, buckets), 1).astype(F32) == hash_col, 1.0, 0.0
    ).astype(BF16)
    index8 = jnp.zeros((8, rows), F32)
    for h in range(heads):
        index8 = jnp.where(sub == h, idx_ref[h].astype(F32), index8)
    rates = jnp.exp2(-0.25 * index8)
    steps = (lax.broadcasted_iota(jnp.int32, (8, rows), 1) + 1).astype(F32)
    cum = count * LOG_KEEP - steps * rates
    total = cum[:, rows - 1:rows]
    msg[:, :buckets] = dot(jnp.exp(total - cum).astype(BF16), hot[...])
    msg[:, buckets:] = jnp.broadcast_to(total, (8, 128))

    sends = []
    for d in range(1, n_ctx):
        sends.append(pltpu.make_async_remote_copy(
            src_ref=msg, dst_ref=msgs.at[d - 1], send_sem=ctx_send.at[d - 1],
            recv_sem=ctx_recv.at[d - 1],
            device_id={"ctx": lax.rem(place + d, n_ctx)}, device_id_type=MESH))
        sends[-1].start()

    gathers[0].wait_recv()
    gathers[5].start()
    gathers[7].start()
    gathers[1].wait_recv()
    gathers[6].start()
    gathers[8].start()
    gathers[3].wait_recv()
    gathers[9].start()
    gathers[4].wait_recv()
    gathers[10].start()

    incoming, passed = jnp.zeros((8, buckets), F32), jnp.zeros((8, 1), F32)
    for d in range(1, n_ctx):
        sends[d - 1].wait_recv()
        reached = jnp.where(d <= place, 1.0, 0.0)
        incoming = incoming + reached * jnp.exp(passed) * msgs[d - 1, :, :buckets]
        passed = passed + msgs[d - 1, :, buckets:buckets + 1]
    incoming_col = incoming.T

    gathers[5].wait_recv()
    gathers[11].start()
    gathers[6].wait_recv()
    gathers[12].start()
    for k in (2, 7, 8, 9, 10, 11, 12):
        gathers[k].wait_recv()

    n_tp = full.shape[0]
    squares = jnp.zeros((buckets, 1), F32)
    for j in range(n_tp):
        x = full[j].astype(F32)
        squares = squares + jnp.sum(x * x, axis=1, keepdims=True)
    inv = lax.rsqrt(squares / model + 1e-05)
    for j in range(n_tp):
        cols = slice(j * width, (j + 1) * width)
        normed[:, cols] = (full[j].astype(F32) * inv * gain_ref[:, cols].astype(F32)).astype(BF16)
    for n in range(tiles):
        loads[n].wait()

    @pl.loop(0, 2 * group)
    def _(n):
        y = dot(normed[...], w_in[n])
        qkv[n] = (y / (1.0 + jnp.exp(-y))).astype(BF16)

    @pl.loop(2 * group, tiles)
    def _(n):
        qkv[n] = dot(normed[...], w_in[n]).astype(BF16)

    for h in range(heads):
        lanes = slice((h % per) * hw, (h % per + 1) * hw)
        key, value = qkv[group + h // per, :, lanes], qkv[2 * group + h // per, :, lanes]
        state[h] = dot_rows((key.astype(F32) * incoming_col[:, h:h + 1]).astype(BF16), value)
    for load in loads[tiles:]:
        load.wait()

    n_chunks = rows // chunk
    part = chunk // 2
    t_at = lax.broadcasted_iota(jnp.int32, (chunk, chunk), 0)
    s_at = lax.broadcasted_iota(jnp.int32, (chunk, chunk), 1)
    ahead = (t_at - s_at).astype(F32)
    step_col = (lax.broadcasted_iota(jnp.int32, (chunk, 1), 0) + 1).astype(F32)

    def rs(k, src, dst, peer):
        return pltpu.make_async_remote_copy(
            src_ref=src, dst_ref=dst, send_sem=rs_send.at[k], recv_sem=rs_recv.at[k],
            device_id={"tp": peer}, device_id_type=MESH)

    stage0 = [rs(5 * c, s0.at[c], r0.at[c], sib) for c in range(n_chunks)]
    stage1 = [[rs(5 * c + 1 + f, s1.at[c, f], r1.at[c, f], (xp, yp)[f]) for f in range(2)]
              for c in range(n_chunks)]
    stage2 = [[rs(5 * c + 3 + f, s2.at[c, f], r2.at[c, f], (yp, xp)[f]) for f in range(2)]
              for c in range(n_chunks)]

    def attend(c):
        at = slice(c * chunk, (c + 1) * chunk)
        one = hot[at]
        picked = [dot(one, qkv[n]).astype(BF16) for n in range(tiles)]
        here_col, here_row = count_col[at], count[0:1, at]
        before = count_col[c * chunk - 1:c * chunk] if c else jnp.zeros((1, 1), F32)
        last = count_col[(c + 1) * chunk - 1:(c + 1) * chunk]
        gap = jnp.where(t_at >= s_at, (here_col - here_row) * LOG_KEEP, -1e30)
        for h in range(heads):
            lanes = slice((h % per) * hw, (h % per + 1) * hw)
            query = picked[h // per][:, lanes]
            key = picked[group + h // per][:, lanes]
            value = picked[2 * group + h // per][:, lanes]
            rate = rates[h:h + 1, 0:1]
            weights = (dot_lanes(query, key) * jnp.exp(gap - ahead * rate)).astype(BF16)
            carried = state[h]
            begun = jnp.exp((here_col - before) * LOG_KEEP - step_col * rate)
            attended = dot(weights, value) + begun * dot(query, carried.astype(BF16))
            if c < n_chunks - 1:
                left = jnp.exp((last - here_col) * LOG_KEEP - (chunk - step_col) * rate)
                decayed = (key.astype(F32) * left).astype(BF16)
                whole = jnp.exp((last - before) * LOG_KEEP - chunk * rate)
                state[h] = whole * carried + dot_rows(decayed, value)
            scale = lax.rsqrt(jnp.mean(attended * attended, axis=1, keepdims=True) + 1e-06)
            wide = slice(h * hw, (h + 1) * hw)
            att[:, wide] = (attended * scale * ogain_ref[:, wide].astype(F32)).astype(BF16)
        for pair in range(2):
            s0[c, pair] = dot(att[...], w_o[pair]).astype(BF16)
        stage0[c].start()
        for pair in range(2):
            keep0[c, pair] = dot(att[...], w_o[2 + pair])

    def after0(c):
        stage0[c].wait_recv()
        for f in range(2):
            cut = slice(f * part, (f + 1) * part)
            sums = [keep0[c, q // 2, cut, (q % 2) * width:(q % 2 + 1) * width]
                    + r0[c, q // 2, cut, (q % 2) * width:(q % 2 + 1) * width].astype(F32)
                    for q in range(4)]
            go, stay = (((1, 3), (0, 2)), ((2, 3), (0, 1)))[f]
            for i in range(2):
                s1[c, f, i] = sums[go[i]].astype(BF16)
                keep1[c, f, i] = sums[stay[i]]
            stage1[c][f].start()

    def after1(c):
        for f in range(2):
            stage1[c][f].wait_recv()
            s2[c, f] = (keep1[c, f, 1] + r1[c, f, 1].astype(F32)).astype(BF16)
            stage2[c][f].start()
            keep2[c, f] = keep1[c, f, 0] + r1[c, f, 0].astype(F32)

    def after2(c):
        for f in range(2):
            stage2[c][f].wait_recv()
            at = slice(c * chunk + f * part, c * chunk + (f + 1) * part)
            residual = dot(hot[at], table_ref[...])
            out_ref[at, :] = (residual + (keep2[c, f] + r2[c, f].astype(F32))).astype(BF16)

    for step in range(n_chunks + 3):
        if step < n_chunks:
            attend(step)
        if 0 <= step - 1 < n_chunks:
            after0(step - 1)
        if 0 <= step - 2 < n_chunks:
            after1(step - 2)
        if 0 <= step - 3 < n_chunks:
            after2(step - 3)

    for copy in gathers + sends:
        copy.wait_send()
    for c in range(n_chunks):
        stage0[c].wait_send()
        for f in range(2):
            stage1[c][f].wait_send()
            stage2[c][f].wait_send()


def per_device(n_ctx, n_tp, token_ids, marks, table, norm_gain, w_query, w_key, w_value, decay_idx, out_gain, w_out):
    if n_tp != len(ORDER):
        raise ValueError("tp size")
    rows, (buckets, width) = token_ids.shape[0], table.shape
    model, columns = w_query.shape
    heads = decay_idx.shape[0]
    hw = columns // heads
    tile = 2 * hw
    tiles = 3 * columns // tile
    chunk = rows // 4
    n_chunks = rows // chunk
    part = chunk // 2
    vmem, hbm = pl.BlockSpec(memory_space=pltpu.VMEM), pl.BlockSpec(memory_space=pl.ANY)
    return pl.pallas_call(
        functools.partial(layer, n_ctx, chunk),
        out_shape=jax.ShapeDtypeStruct((rows, width), BF16),
        in_specs=[vmem, vmem, vmem, vmem, hbm, hbm, hbm,
                  pl.BlockSpec(memory_space=pltpu.SMEM), vmem, hbm],
        out_specs=vmem,
        scratch_shapes=[
            pltpu.VMEM((n_tp, buckets, width), BF16),
            pltpu.VMEM((buckets, model), BF16),
            pltpu.VMEM((tiles, model, tile), BF16),
            pltpu.VMEM((n_tp // 2, columns, 2 * width), BF16),
            pltpu.VMEM((tiles, buckets, tile), BF16),
            pltpu.VMEM((rows, buckets), BF16),
            pltpu.VMEM((heads, hw, hw), F32),
            pltpu.VMEM((8, buckets + 128), F32),
            pltpu.VMEM((max(n_ctx - 1, 1), 8, buckets + 128), F32),
            pltpu.VMEM((chunk, columns), BF16),
            pltpu.VMEM((n_chunks, 2, chunk, 2 * width), F32),
            pltpu.VMEM((n_chunks, 2, chunk, 2 * width), BF16),
            pltpu.VMEM((n_chunks, 2, chunk, 2 * width), BF16),
            pltpu.VMEM((n_chunks, 2, 2, part, width), F32),
            pltpu.VMEM((n_chunks, 2, 2, part, width), BF16),
            pltpu.VMEM((n_chunks, 2, 2, part, width), BF16),
            pltpu.VMEM((n_chunks, 2, part, width), F32),
            pltpu.VMEM((n_chunks, 2, part, width), BF16),
            pltpu.VMEM((n_chunks, 2, part, width), BF16),
            pltpu.SemaphoreType.DMA((tiles + n_tp,)),
            pltpu.SemaphoreType.DMA((13,)),
            pltpu.SemaphoreType.DMA((13,)),
            pltpu.SemaphoreType.DMA((max(n_ctx - 1, 1),)),
            pltpu.SemaphoreType.DMA((max(n_ctx - 1, 1),)),
            pltpu.SemaphoreType.DMA((5 * n_chunks,)),
            pltpu.SemaphoreType.DMA((5 * n_chunks,)),
        ],
        compiler_params=pltpu.CompilerParams(
            collective_id=0, has_side_effects=True, vmem_limit_bytes=56 * 2**20),
        name="layer",
    )(
        token_ids.reshape(1, rows), marks.reshape(1, rows), table, norm_gain.reshape(1, model),
        w_query, w_key, w_value, decay_idx, out_gain.reshape(1, columns), w_out,
    )


def solution(mesh):
    return jax.shard_map(
        functools.partial(per_device, mesh.shape["ctx"], mesh.shape["tp"]),
        mesh=mesh,
        in_specs=(
            P("ctx"), P("ctx"), P(None, "tp"), P(), P(None, "tp"), P(None, "tp"), P(None, "tp"),
            P("tp"), P("tp"), P("tp", None),
        ),
        out_specs=P("ctx", "tp"),
        check_vma=False,
    )
```

```python
import functools
import math

import jax
import jax.numpy as jnp
from jax import lax
from jax.experimental import pallas as pl
from jax.experimental.pallas import tpu as pltpu
from jax.sharding import PartitionSpec as P

MESH = pl.DeviceIdType.MESH
LOG_KEEP = math.log(0.75)
F32, BF16 = jnp.float32, jnp.bfloat16
ORDER = (1, 3, 5, 7, 0, 2, 4, 6)


def dot(a, b):
    return jnp.dot(a, b, preferred_element_type=F32)


def dot_rows(a, b):
    return lax.dot_general(a, b, (((0,), (0,)), ((), ())), preferred_element_type=F32)


def dot_lanes(a, b):
    return lax.dot_general(a, b, (((1,), (1,)), ((), ())), preferred_element_type=F32)


def layer(
    n_ctx, chunk,
    ids_ref, marks_ref, table_ref, gain_ref, wq_ref, wk_ref, wv_ref, idx_ref, ogain_ref, wout_ref,
    out_ref,
    sq_out, sq_in, full, gains, normed, acc, w_in, w_o, qkv, hot, state, msg, msgs, att, keep0, s0, r0, keep1, s1, r1, keep2, s2, r2,
    sq_send, sq_recv, load_sem, ag_send, ag_recv, ctx_send, ctx_recv, rs_send, rs_recv,
):
    me, place = lax.axis_index("tp"), lax.axis_index("ctx")
    buckets, width = table_ref.shape
    rows = ids_ref.shape[1]
    tiles, model, tile = w_in.shape
    heads, hw = state.shape[0], state.shape[1]
    per = tile // hw
    group = heads // per
    bits = [(me // (1 << k)) % 2 for k in range(3)]

    def other(p):
        index = me
        for k in range(3):
            if (p >> k) & 1:
                index = index + (1 - 2 * bits[k]) * (1 << k)
        return index

    sib, xp, yp, diag = other(1), other(2), other(4), other(6)

    barrier = pltpu.get_barrier_semaphore()
    n_tp = full.shape[0]
    for d in range(1, n_tp):
        pl.semaphore_signal(
            barrier, inc=1, device_id={"tp": lax.rem(me + d, n_tp)}, device_id_type=MESH)
    for d in range(1, n_ctx):
        pl.semaphore_signal(
            barrier, inc=1, device_id={"ctx": lax.rem(place + d, n_ctx)}, device_id_type=MESH)
    loads = []
    for n in range(tiles):
        source = (wq_ref, wk_ref, wv_ref)[n // group]
        loads.append(pltpu.make_async_copy(
            source.at[:, pl.ds((n % group) * tile, tile)], w_in.at[n], load_sem.at[n]))
    for at, p in enumerate(ORDER):
        first = pl.multiple_of(other(p) * width, 128)
        loads.append(pltpu.make_async_copy(
            wout_ref.at[:, pl.ds(first, width)],
            w_o.at[at // 2, :, pl.ds((at % 2) * width, width)], load_sem.at[tiles + at]))
    for load in loads:
        load.start()

    own = table_ref[...].astype(F32)
    sq_out[...] = jnp.broadcast_to(
        jnp.sum(own * own, axis=1, keepdims=True), (buckets, 128)).T[:8]
    pl.semaphore_wait(barrier, n_tp - 1 + n_ctx - 1)

    half = buckets // 2
    lo, hi = pl.ds(0, half), pl.ds(half, half)

    def ag(k, src, dst, peer):
        return pltpu.make_async_remote_copy(
            src_ref=src, dst_ref=dst, send_sem=ag_send.at[k], recv_sem=ag_recv.at[k],
            device_id={"tp": peer}, device_id_type=MESH)

    gathers = [
        ag(0, table_ref.at[lo], full.at[me, lo], xp),
        ag(1, table_ref.at[hi], full.at[me, hi], yp),
        ag(2, table_ref, full.at[me], sib),
        ag(3, table_ref.at[hi], full.at[me, hi], xp),
        ag(4, table_ref.at[lo], full.at[me, lo], yp),
        ag(5, full.at[xp, lo], full.at[xp, lo], yp),
        ag(6, full.at[yp, hi], full.at[yp, hi], xp),
        ag(7, full.at[xp, lo], full.at[xp, lo], sib),
        ag(8, full.at[yp, hi], full.at[yp, hi], sib),
        ag(9, full.at[xp, hi], full.at[xp, hi], sib),
        ag(10, full.at[yp, lo], full.at[yp, lo], sib),
        ag(11, full.at[diag, lo], full.at[diag, lo], sib),
        ag(12, full.at[diag, hi], full.at[diag, hi], sib),
    ]
    for k in range(3):
        gathers[k].start()
    shares = []
    for d in range(1, n_tp):
        shares.append(pltpu.make_async_remote_copy(
            src_ref=sq_out, dst_ref=sq_in.at[d - 1], send_sem=sq_send.at[d - 1],
            recv_sem=sq_recv.at[d - 1],
            device_id={"tp": lax.rem(me + d, n_tp)}, device_id_type=MESH))
        shares[-1].start()
    full[me] = table_ref[...]
    for j in range(n_tp):
        gains[j] = gain_ref[j * width:(j + 1) * width].astype(F32).reshape(1, width)

    for k in (3, 4):
        gathers[k].start()

    hashed = ((ids_ref[...] * 7919 + 13) & (buckets - 1)).astype(F32)
    upto = lax.broadcasted_iota(jnp.int32, (rows, rows), 0) <= lax.broadcasted_iota(
        jnp.int32, (rows, rows), 1)
    mark8 = jnp.broadcast_to(marks_ref[...].astype(F32), (8, rows)).astype(BF16)
    count = dot(mark8, jnp.where(upto, 1.0, 0.0).astype(BF16))
    sub = lax.broadcasted_iota(jnp.int32, (8, rows), 0)
    turned = jnp.where(sub == 0, jnp.broadcast_to(hashed, (8, rows)), count).T
    hash_col, count_col = turned[:, 0:1], turned[:, 1:2]
    hot[...] = jnp.where(
        lax.broadcasted_iota(jnp.int32, (rows, buckets), 1).astype(F32) == hash_col, 1.0, 0.0
    ).astype(BF16)
    index8 = jnp.zeros((8, rows), F32)
    for h in range(heads):
        index8 = jnp.where(sub == h, idx_ref[h].astype(F32), index8)
    rates = jnp.exp2(-0.25 * index8)
    steps = (lax.broadcasted_iota(jnp.int32, (8, rows), 1) + 1).astype(F32)
    cum = count * LOG_KEEP - steps * rates
    total = cum[:, rows - 1:rows]
    msg[:, :buckets] = dot(jnp.exp(total - cum).astype(BF16), hot[...])
    msg[:, buckets:] = jnp.broadcast_to(total, (8, 128))

    sends = []
    for d in range(1, n_ctx):
        sends.append(pltpu.make_async_remote_copy(
            src_ref=msg, dst_ref=msgs.at[d - 1], send_sem=ctx_send.at[d - 1],
            recv_sem=ctx_recv.at[d - 1],
            device_id={"ctx": lax.rem(place + d, n_ctx)}, device_id_type=MESH))
        sends[-1].start()

    def scale(block, k):
        first = block - bits[0]
        for i in range(2):
            x = full[first + i].astype(F32)
            normed[k, :, i * width:(i + 1) * width] = (x * inv * gains[first + i]).astype(BF16)
        return pl.ds(pl.multiple_of(first * width, 128), 2 * width)

    gathers[0].wait_recv()
    gathers[5].start()
    gathers[7].start()
    gathers[1].wait_recv()
    gathers[6].start()
    gathers[8].start()
    squares = sq_out[...]
    for d in range(1, n_tp):
        shares[d - 1].wait_recv()
        squares = squares + sq_in[d - 1]
    inv_row = lax.rsqrt(squares / model + 1e-05)
    inv = jnp.broadcast_to(inv_row[0:1], (128, buckets)).T[:, 0:1]
    gathers[2].wait_recv()
    span = scale(me, 0)
    for n in range(tiles):
        loads[n].wait()

    @pl.loop(0, tiles)
    def _(n):
        acc[n] = dot(normed[0], w_in[n, span])

    gathers[3].wait_recv()
    gathers[9].start()
    gathers[4].wait_recv()
    gathers[10].start()

    incoming, passed = jnp.zeros((8, buckets), F32), jnp.zeros((8, 1), F32)
    for d in range(1, n_ctx):
        sends[d - 1].wait_recv()
        reached = jnp.where(d <= place, 1.0, 0.0)
        incoming = incoming + reached * jnp.exp(passed) * msgs[d - 1, :, :buckets]
        passed = passed + msgs[d - 1, :, buckets:buckets + 1]
    incoming_col = incoming.T

    gathers[7].wait_recv()
    gathers[9].wait_recv()
    span1 = scale(xp, 1)

    @pl.loop(0, tiles)
    def _(n):
        acc[n] += dot(normed[1], w_in[n, span1])

    gathers[5].wait_recv()
    gathers[11].start()
    gathers[6].wait_recv()
    gathers[12].start()
    gathers[8].wait_recv()
    gathers[10].wait_recv()
    span2 = scale(yp, 0)

    @pl.loop(0, tiles)
    def _(n):
        acc[n] += dot(normed[0], w_in[n, span2])

    gathers[11].wait_recv()
    gathers[12].wait_recv()
    span3 = scale(diag, 1)

    @pl.loop(0, 2 * group)
    def _(n):
        y = acc[n] + dot(normed[1], w_in[n, span3])
        qkv[n] = (y / (1.0 + jnp.exp(-y))).astype(BF16)

    @pl.loop(2 * group, tiles)
    def _(n):
        qkv[n] = (acc[n] + dot(normed[1], w_in[n, span3])).astype(BF16)

    for h in range(heads):
        lanes = slice((h % per) * hw, (h % per + 1) * hw)
        key, value = qkv[group + h // per, :, lanes], qkv[2 * group + h // per, :, lanes]
        state[h] = dot_rows((key.astype(F32) * incoming_col[:, h:h + 1]).astype(BF16), value)
    for load in loads[tiles:]:
        load.wait()

    n_chunks = rows // chunk
    part = chunk // 2
    t_at = lax.broadcasted_iota(jnp.int32, (chunk, chunk), 0)
    s_at = lax.broadcasted_iota(jnp.int32, (chunk, chunk), 1)
    ahead = (t_at - s_at).astype(F32)
    step_col = (lax.broadcasted_iota(jnp.int32, (chunk, 1), 0) + 1).astype(F32)

    def rs(k, src, dst, peer):
        return pltpu.make_async_remote_copy(
            src_ref=src, dst_ref=dst, send_sem=rs_send.at[k], recv_sem=rs_recv.at[k],
            device_id={"tp": peer}, device_id_type=MESH)

    stage0 = [rs(5 * c, s0.at[c], r0.at[c], sib) for c in range(n_chunks)]
    stage1 = [[rs(5 * c + 1 + f, s1.at[c, f], r1.at[c, f], (xp, yp)[f]) for f in range(2)]
              for c in range(n_chunks)]
    stage2 = [[rs(5 * c + 3 + f, s2.at[c, f], r2.at[c, f], (yp, xp)[f]) for f in range(2)]
              for c in range(n_chunks)]

    def attend(c):
        at = slice(c * chunk, (c + 1) * chunk)
        one = hot[at]
        picked = [dot(one, qkv[n]).astype(BF16) for n in range(tiles)]
        here_col, here_row = count_col[at], count[0:1, at]
        before = count_col[c * chunk - 1:c * chunk] if c else jnp.zeros((1, 1), F32)
        last = count_col[(c + 1) * chunk - 1:(c + 1) * chunk]
        gap = jnp.where(t_at >= s_at, (here_col - here_row) * LOG_KEEP, -1e30)
        for h in range(heads):
            lanes = slice((h % per) * hw, (h % per + 1) * hw)
            query = picked[h // per][:, lanes]
            key = picked[group + h // per][:, lanes]
            value = picked[2 * group + h // per][:, lanes]
            rate = rates[h:h + 1, 0:1]
            weights = (dot_lanes(query, key) * jnp.exp(gap - ahead * rate)).astype(BF16)
            carried = state[h]
            begun = jnp.exp((here_col - before) * LOG_KEEP - step_col * rate)
            attended = dot(weights, value) + begun * dot(query, carried.astype(BF16))
            if c < n_chunks - 1:
                left = jnp.exp((last - here_col) * LOG_KEEP - (chunk - step_col) * rate)
                decayed = (key.astype(F32) * left).astype(BF16)
                whole = jnp.exp((last - before) * LOG_KEEP - chunk * rate)
                state[h] = whole * carried + dot_rows(decayed, value)
            scale = lax.rsqrt(jnp.mean(attended * attended, axis=1, keepdims=True) + 1e-06)
            wide = slice(h * hw, (h + 1) * hw)
            att[:, wide] = (attended * scale * ogain_ref[wide].astype(F32).reshape(1, hw)).astype(BF16)
        for pair in range(2):
            s0[c, pair] = dot(att[...], w_o[pair]).astype(BF16)
        stage0[c].start()
        for pair in range(2):
            keep0[c, pair] = dot(att[...], w_o[2 + pair])

    def after0(c):
        stage0[c].wait_recv()
        for f in range(2):
            cut = slice(f * part, (f + 1) * part)
            sums = [keep0[c, q // 2, cut, (q % 2) * width:(q % 2 + 1) * width]
                    + r0[c, q // 2, cut, (q % 2) * width:(q % 2 + 1) * width].astype(F32)
                    for q in range(4)]
            go, stay = (((1, 3), (0, 2)), ((2, 3), (0, 1)))[f]
            for i in range(2):
                s1[c, f, i] = sums[go[i]].astype(BF16)
                keep1[c, f, i] = sums[stay[i]]
            stage1[c][f].start()

    def after1(c):
        for f in range(2):
            stage1[c][f].wait_recv()
            s2[c, f] = (keep1[c, f, 1] + r1[c, f, 1].astype(F32)).astype(BF16)
            stage2[c][f].start()
            keep2[c, f] = keep1[c, f, 0] + r1[c, f, 0].astype(F32)

    def after2(c):
        for f in range(2):
            stage2[c][f].wait_recv()
            at = slice(c * chunk + f * part, c * chunk + (f + 1) * part)
            residual = dot(hot[at], table_ref[...])
            out_ref[at, :] = (residual + (keep2[c, f] + r2[c, f].astype(F32))).astype(BF16)

    for step in range(n_chunks + 3):
        if step < n_chunks:
            attend(step)
        if 0 <= step - 1 < n_chunks:
            after0(step - 1)
        if 0 <= step - 2 < n_chunks:
            after1(step - 2)
        if 0 <= step - 3 < n_chunks:
            after2(step - 3)

    for copy in gathers + sends + shares:
        copy.wait_send()
    for c in range(n_chunks):
        stage0[c].wait_send()
        for f in range(2):
            stage1[c][f].wait_send()
            stage2[c][f].wait_send()


def per_device(n_ctx, n_tp, token_ids, marks, table, norm_gain, w_query, w_key, w_value, decay_idx, out_gain, w_out):
    if n_tp != len(ORDER):
        raise ValueError("tp size")
    rows, (buckets, width) = token_ids.shape[0], table.shape
    model, columns = w_query.shape
    heads = decay_idx.shape[0]
    hw = columns // heads
    tile = 2 * hw
    tiles = 3 * columns // tile
    chunk = rows // 4
    n_chunks = rows // chunk
    part = chunk // 2
    vmem, hbm = pl.BlockSpec(memory_space=pltpu.VMEM), pl.BlockSpec(memory_space=pl.ANY)
    return pl.pallas_call(
        functools.partial(layer, n_ctx, chunk),
        out_shape=jax.ShapeDtypeStruct((rows, width), BF16),
        in_specs=[vmem, vmem, vmem, vmem, hbm, hbm, hbm,
                  pl.BlockSpec(memory_space=pltpu.SMEM), vmem, hbm],
        out_specs=vmem,
        scratch_shapes=[
            pltpu.VMEM((8, buckets), F32),
            pltpu.VMEM((n_tp - 1, 8, buckets), F32),
            pltpu.VMEM((n_tp, buckets, width), BF16),
            pltpu.VMEM((n_tp, 1, width), F32),
            pltpu.VMEM((2, buckets, 2 * width), BF16),
            pltpu.VMEM((tiles, buckets, tile), F32),
            pltpu.VMEM((tiles, model, tile), BF16),
            pltpu.VMEM((n_tp // 2, columns, 2 * width), BF16),
            pltpu.VMEM((tiles, buckets, tile), BF16),
            pltpu.VMEM((rows, buckets), BF16),
            pltpu.VMEM((heads, hw, hw), F32),
            pltpu.VMEM((8, buckets + 128), F32),
            pltpu.VMEM((max(n_ctx - 1, 1), 8, buckets + 128), F32),
            pltpu.VMEM((chunk, columns), BF16),
            pltpu.VMEM((n_chunks, 2, chunk, 2 * width), F32),
            pltpu.VMEM((n_chunks, 2, chunk, 2 * width), BF16),
            pltpu.VMEM((n_chunks, 2, chunk, 2 * width), BF16),
            pltpu.VMEM((n_chunks, 2, 2, part, width), F32),
            pltpu.VMEM((n_chunks, 2, 2, part, width), BF16),
            pltpu.VMEM((n_chunks, 2, 2, part, width), BF16),
            pltpu.VMEM((n_chunks, 2, part, width), F32),
            pltpu.VMEM((n_chunks, 2, part, width), BF16),
            pltpu.VMEM((n_chunks, 2, part, width), BF16),
            pltpu.SemaphoreType.DMA((n_tp - 1,)),
            pltpu.SemaphoreType.DMA((n_tp - 1,)),
            pltpu.SemaphoreType.DMA((tiles + n_tp,)),
            pltpu.SemaphoreType.DMA((13,)),
            pltpu.SemaphoreType.DMA((13,)),
            pltpu.SemaphoreType.DMA((max(n_ctx - 1, 1),)),
            pltpu.SemaphoreType.DMA((max(n_ctx - 1, 1),)),
            pltpu.SemaphoreType.DMA((5 * n_chunks,)),
            pltpu.SemaphoreType.DMA((5 * n_chunks,)),
        ],
        compiler_params=pltpu.CompilerParams(
            collective_id=0, has_side_effects=True, vmem_limit_bytes=56 * 2**20),
        name="layer",
    )(
        token_ids.reshape(1, rows), marks.reshape(1, rows), table, norm_gain,
        w_query, w_key, w_value, decay_idx, out_gain, w_out,
    )


def solution(mesh):
    return jax.shard_map(
        functools.partial(per_device, mesh.shape["ctx"], mesh.shape["tp"]),
        mesh=mesh,
        in_specs=(
            P("ctx"), P("ctx"), P(None, "tp"), P(), P(None, "tp"), P(None, "tp"), P(None, "tp"),
            P("tp"), P("tp"), P("tp", None),
        ),
        out_specs=P("ctx", "tp"),
        check_vma=False,
    )
```
